32 devices in a mesh: ga: 2 (over y), col: 16 (over z, x, core).
Axes of the slice: x: 2, y: 2, z: 4, core: 2. Of those that a mesh axis runs over, the one named last changes fastest.
Arguments:
- query_nope: bfloat16 [128, 4096], P(('ga', 'col')), parts along dimension 0, may hold values from -6 to 6
- query_rope: bfloat16 [128, 2048], P(('ga', 'col')), parts along dimension 0, may hold values from -104 to 104, as said below
- cache: bfloat16 [8192, 576], P(('ga', 'col')), parts along dimension 0, may hold values from -6 to 6, as said below
- key_docs: int32 [8192], P(('ga', 'col')), parts along dimension 0, may hold values from 0 to 7, as said below
- query_docs: int32 [128], P(('ga', 'col')), parts along dimension 0, may hold values from 0 to 7, as said below
- query_pos: int32 [128], P(('ga', 'col')), parts along dimension 0, may hold values from 1 to 4095, as said below
- w_uk: bfloat16 [512, 4096], replicated, may hold values from -0.25 to 0.25
- w_uv: bfloat16 [512, 4096], replicated, may hold values from -0.25 to 0.25
Outputs:
- attended: bfloat16 [128, 4096], P(('ga', 'col')), parts along dimension 0
The draws below stay inside these ranges and needn't reach their ends.
There are 2 independent parts, one for each index of `ga`. The reference program is written for one: setup_inputs(seed, part) draws one part's arguments, and reference() takes and returns one part's arrays. A program takes and returns all parts, laid end to end along the dimension named above; an argument that names none is the same for every part. Nothing has to cross between parts.
Inputs may be any that keep to these rules, and one draw needn't show every extreme that they name: `key_docs`: ids start at 0 and never fall along the cache; a document is a run of equal ids; eight documents. query_docs[i] equals key_docs[query_pos[i]]. `query_pos`: a position from 1 to 4095, never the first token of a document. `query_rope`: real values. `cache`: real values.
All inputs are finite; a program needn't handle non-finite values.
Results may differ from the reference program's by a relative error of at most 0.001.
Values may be sent and summed in bfloat16 or wider, within the bound.
No kernel may reach another device: no remote copies, remote signals or barrier semaphores. Data moves between devices by JAX's collectives and lax.ppermute only.
A program may use at most 192 MiB of HBM per device.

```python
import math
import jax
import jax.numpy as jnp
from jax import lax

H = 32
DN = 128
DR = 64
DV = 128
R = 512
CACHE = 4096
QUERIES = 64


def layout_ints(key):
    base_key = jax.random.fold_in(key, 11)
    first_key, second_key = jax.random.split(base_key)
    halves = jax.random.permutation(first_key, CACHE // 2 - 1)[:7].astype(jnp.int32)
    bounds = 2 * (halves + 1)
    flags = jnp.zeros((CACHE,), jnp.int32).at[bounds].set(1)
    documents = jnp.cumsum(flags).astype(jnp.int32)
    positions = jax.random.randint(second_key, (QUERIES,), 1, CACHE).astype(jnp.int32)
    positions = jnp.where(flags[positions] == 1, positions - 1, positions).astype(jnp.int32)
    positions = positions.at[0].set(CACHE - 1)
    positions = positions.at[1].set(1)
    return (documents, positions, documents[positions])


def float_parts(key):
    float_key = jax.random.fold_in(key, 23)
    cache_key, rope_key = jax.random.split(float_key)
    table = jnp.clip(jax.random.normal(cache_key, (CACHE, R + DR), jnp.float32), -6.0, 6.0)
    turned = jnp.clip(jax.random.normal(rope_key, (QUERIES, H * DR), jnp.float32), -6.0, 6.0)
    return (table, turned)


def draw_cache(key, part):
    return float_parts(key)[0].astype(jnp.bfloat16)


def draw_query_rope(key, part):
    return float_parts(key)[1].astype(jnp.bfloat16)


def draw_key_docs(key, part):
    return layout_ints(key)[0]


def draw_query_pos(key, part):
    return layout_ints(key)[1]


def draw_query_docs(key, part):
    return layout_ints(key)[2]


def block_scale(stream_key, shape, shards, low, high):
    def one(dim, blocks):
        heights = jax.random.uniform(jax.random.fold_in(jax.random.fold_in(stream_key, 6), dim), (blocks,), jnp.float32, low / len(shards), high / len(shards))
        return jnp.repeat(jnp.exp(heights), shape[dim] // blocks).reshape((-1,) + (1,) * (len(shape) - dim - 1))

    loudness = one(*shards[0])
    for cut in shards[1:]:
        loudness = loudness * one(*cut)
    return loudness


def noise(own_key, extent, scale, limit, shards=(), kind=jnp.bfloat16):
    drawn = jax.random.normal(own_key, extent, jnp.float32) * scale
    if len(shards) > 0:
        drawn = block_scale(own_key, extent, shards, -0.22, 0.18) * drawn
    return jnp.clip(drawn, min=-limit, max=limit).astype(kind)


def setup_inputs(seed: int = 0, part: int = 0) -> dict:
    seeds = jax.random.split(jax.random.key(seed), 9)
    part_splits = jax.random.split(jax.random.fold_in(seeds[8], part), 9)
    query_nope = noise(part_splits[0], (QUERIES, H * DN), 1.0, 6.0, ((0, 16),))
    query_rope = draw_query_rope(jax.random.fold_in(jax.random.fold_in(seeds[8], part), 71), part)
    cache = draw_cache(jax.random.fold_in(jax.random.fold_in(seeds[8], part), 71), part)
    key_docs = draw_key_docs(jax.random.fold_in(jax.random.fold_in(seeds[8], part), 71), part)
    query_docs = draw_query_docs(jax.random.fold_in(jax.random.fold_in(seeds[8], part), 71), part)
    query_pos = draw_query_pos(jax.random.fold_in(jax.random.fold_in(seeds[8], part), 71), part)
    w_uk = noise(seeds[6], (R, H * DN), R ** -0.5, 0.25)
    w_uv = noise(seeds[7], (R, H * DV), R ** -0.5, 0.25)
    return dict(query_nope=query_nope, query_rope=query_rope, cache=cache, key_docs=key_docs, query_docs=query_docs, query_pos=query_pos, w_uk=w_uk, w_uv=w_uv)


def reference(query_nope, query_rope, cache, key_docs, query_docs, query_pos, w_uk, w_uv):
    scale = 1.0 / math.sqrt(DN + DR)
    highest = lax.Precision.HIGHEST
    latent = cache[:, :R].astype(jnp.float32)
    krope = cache[:, R:].astype(jnp.float32)
    key_place = jnp.arange(CACHE, dtype=jnp.int32)
    visible = (key_docs[None, :] == query_docs[:, None]) & (key_place[None, :] <= query_pos[:, None])
    wide_keys = w_uk.astype(jnp.float32)
    wide_vals = w_uv.astype(jnp.float32)
    q_nope_all = query_nope.astype(jnp.float32)
    q_rope_all = query_rope.astype(jnp.float32)

    def one_head(head):
        w_key = lax.dynamic_slice_in_dim(wide_keys, (head * DN).astype(jnp.int32), DN, 1)
        w_val = lax.dynamic_slice_in_dim(wide_vals, (head * DV).astype(jnp.int32), DV, 1)
        keys = jnp.dot(latent, w_key, precision=highest)
        values = jnp.dot(latent, w_val, precision=highest)
        q_flat = lax.dynamic_slice_in_dim(q_nope_all, (head * DN).astype(jnp.int32), DN, 1)
        q_turn = lax.dynamic_slice_in_dim(q_rope_all, (head * DR).astype(jnp.int32), DR, 1)
        scores = jnp.dot(q_flat, keys.T, precision=highest)
        scores = (scores + jnp.dot(q_turn, krope.T, precision=highest)) * scale
        scores = jnp.where(visible, scores, -1e+30)
        top = lax.optimization_barrier(jnp.max(scores, axis=1, keepdims=True))
        weights = jnp.where(visible, jnp.exp(scores - top), 0.0)
        numer = jnp.dot(weights, values, precision=highest)
        return numer / lax.optimization_barrier(jnp.sum(weights, axis=1, keepdims=True))
    result = lax.map(one_head, jnp.arange(H, dtype=jnp.int32))
    return result.transpose(1, 0, 2).reshape(QUERIES, H * DV).astype(jnp.bfloat16)
```

```python
import math

import jax
import jax.numpy as jnp
from jax import lax
from jax.sharding import PartitionSpec as P

H = 32
DN = 128
DR = 64
DV = 128
R = 512
META = 128


def split(x):
    high = lax.reduce_precision(x, 8, 7)
    return high.astype(jnp.bfloat16), (x - high).astype(jnp.bfloat16)


def shards(size, query_nope, query_rope, cache, key_docs, query_docs, query_pos, w_uk, w_uv):
    scale = 1.0 / math.sqrt(DN + DR)
    near = math.gcd(size, 4)
    far = size // near
    own_rows = query_nope.shape[0]
    tokens = cache.shape[0]
    me = lax.axis_index("col")

    def swap(x, mask):
        return lax.ppermute(x, "col", [(i, i ^ mask) for i in range(size)])

    blocks, docs = [cache], [key_docs]
    step = 1
    while step < near:
        blocks = blocks + [swap(b, step) for b in blocks]
        docs = docs + [swap(d, step) for d in docs]
        step *= 2
    keys = jnp.concatenate(blocks, axis=0)
    key_doc = jnp.concatenate(docs, axis=0)
    places = [((me ^ k) * tokens) + jnp.arange(tokens, dtype=jnp.int32) for k in range(near)]
    key_place = jnp.concatenate(places, axis=0)

    meta = jnp.stack(
        [query_docs, lax.shift_right_logical(query_pos, 8), lax.bitwise_and(query_pos, 255)], axis=1
    ).astype(jnp.bfloat16)
    meta = jnp.pad(meta, ((0, 0), (0, META - 3)))
    mine = jnp.concatenate([query_nope, query_rope, meta], axis=1)
    groups = [mine] + [swap(mine, near * k) for k in range(1, far)]
    query = jnp.concatenate(groups, axis=0)
    rows = far * own_rows
    q_nope = query[:, : H * DN].reshape(rows, H, DN)
    q_rope = query[:, H * DN : H * (DN + DR)].reshape(rows, H, DR)
    meta = query[:, H * (DN + DR) :].astype(jnp.int32)
    q_doc = meta[:, 0]
    q_pos = meta[:, 1] * 256 + meta[:, 2]

    absorbed = jnp.einsum(
        "qhd,rhd->qhr", q_nope, w_uk.reshape(R, H, DN), preferred_element_type=jnp.float32
    )
    high, low = split(absorbed)
    high = jnp.concatenate([high, q_rope], axis=2)
    low = jnp.concatenate([low, jnp.zeros_like(q_rope)], axis=2)
    both = jnp.stack([high, low]).reshape(2 * rows * H, R + DR)
    scores = jnp.einsum("rc,kc->rk", both, keys, preferred_element_type=jnp.float32)
    scores = scores.reshape(2, rows, H, near * tokens)
    scores = (scores[0] + scores[1]) * scale
    visible = (key_doc[None, :] == q_doc[:, None]) & (key_place[None, :] <= q_pos[:, None])
    scores = jnp.where(visible[:, None, :], scores, -1e30)
    best = jnp.max(scores, axis=2)
    weights = jnp.where(visible[:, None, :], jnp.exp(scores - best[:, :, None]), 0.0)
    total = jnp.sum(weights, axis=2)
    high, low = split(weights)
    both = jnp.stack([high, low]).reshape(2 * rows * H, near * tokens)
    mixed = jnp.dot(both, keys[:, :R], preferred_element_type=jnp.float32)
    mixed = mixed.reshape(2, rows, H, R)
    high, low = split(mixed[0] + mixed[1])
    both = jnp.stack([high, low]).reshape(2 * rows, H, R)
    part = jnp.einsum(
        "qhr,rhv->qhv", both, w_uv.reshape(R, H, DV), preferred_element_type=jnp.float32
    )
    part = part.reshape(2, rows, H * DV)
    part = jnp.concatenate([part[0] + part[1], best, total], axis=1)

    parts = [part[:own_rows]]
    for k in range(1, far):
        parts.append(swap(part[k * own_rows : (k + 1) * own_rows], near * k))
    parts = jnp.stack(parts)
    value = parts[:, :, : H * DV].reshape(far, own_rows, H, DV)
    best = parts[:, :, H * DV : H * DV + H]
    total = parts[:, :, H * DV + H :]
    factor = jnp.exp(best - jnp.max(best, axis=0))
    total = jnp.sum(total * factor, axis=0)
    result = jnp.sum(value * factor[..., None], axis=0) / total[..., None]
    return result.reshape(own_rows, H * DV).astype(jnp.bfloat16)


def solution(mesh):
    split_rows = P(("ga", "col"), None)
    split_flat = P(("ga", "col"))
    placed = (split_rows, split_rows, split_rows, split_flat, split_flat, split_flat, P(), P())
    size = mesh.shape["col"]

    def body(*arrays):
        return shards(size, *arrays)

    return jax.shard_map(body, mesh=mesh, in_specs=placed, out_specs=split_rows, check_vma=False)
```

```python
import functools
import math

import jax
import jax.numpy as jnp
from jax import lax
from jax.experimental import pallas as pl
from jax.experimental.pallas import tpu as pltpu
from jax.sharding import PartitionSpec as P

H = 32
DN = 128
DR = 64
DV = 128
R = 512
META = 128
PAIRS = H // 2
HIDDEN = -1e30
FLOOR = -1e29
VMEM = pl.BlockSpec(memory_space=pltpu.VMEM)
SMEM = pl.BlockSpec(memory_space=pltpu.SMEM)
PARAMS = pltpu.CompilerParams(vmem_limit_bytes=24 * 1024 * 1024)


def iota(shape, axis):
    return lax.broadcasted_iota(jnp.int32, shape, axis)


def split(x):
    high = x.astype(jnp.bfloat16).astype(jnp.float32)
    return high, x - high


def diagonal(x):
    wide = jnp.concatenate([x, x], axis=0)
    own, half = x.shape[0], x.shape[1] // 2
    keep = (iota(wide.shape, 0) // own) == (iota(wide.shape, 1) // half)
    return jnp.where(keep, wide, 0.0)


def absorb_kernel(count, *refs):
    queries, w_ref, a_ref, r_ref = refs[:count], refs[count], refs[count + 1], refs[count + 2]
    half = a_ref.shape[1] // 2
    step = 2 * half // PAIRS
    for duo in range(PAIRS // 2):
        found = []
        for pair in (2 * duo, 2 * duo + 1):
            cols = slice(pair * 2 * DN, (pair + 1) * 2 * DN)
            lhs = [diagonal(q[:, cols].astype(jnp.float32)) for q in queries]
            lhs = jnp.concatenate(lhs, axis=0).astype(jnp.bfloat16)
            found.append(
                lax.dot_general(
                    lhs, w_ref[:, cols], (((1,), (1,)), ((), ())), preferred_element_type=jnp.float32
                )
            )
        rows = slice(duo * step, (duo + 1) * step)
        low_rows = slice(half + duo * step, half + (duo + 1) * step)
        small = step // 2
        for g in range(count):
            own = slice(g * small, (g + 1) * small)
            high, low = split(jnp.concatenate([f[own] for f in found], axis=0))
            a_ref[g, rows] = high.astype(jnp.bfloat16)
            a_ref[g, low_rows] = low.astype(jnp.bfloat16)
            turned = []
            for pair in (2 * duo, 2 * duo + 1):
                cols = slice(H * DN + pair * 2 * DR, H * DN + (pair + 1) * 2 * DR)
                turned.append(diagonal(queries[g][:, cols].astype(jnp.float32)))
            r_ref[g, rows] = jnp.concatenate(turned, axis=0).astype(jnp.bfloat16)


def absorb(queries, w_uk):
    count = len(queries)
    rows = queries[0].shape[0] * H
    return pl.pallas_call(
        functools.partial(absorb_kernel, count),
        out_shape=(
            jax.ShapeDtypeStruct((count, 2 * rows, R), jnp.bfloat16),
            jax.ShapeDtypeStruct((count, rows, 2 * DR), jnp.bfloat16),
        ),
        in_specs=[VMEM] * (count + 1),
        out_specs=(VMEM, VMEM),
        compiler_params=PARAMS,
        name="absorb",
    )(*queries, w_uk)


def attend_kernel(near, me_ref, a_ref, r_ref, q_ref, w_ref, *refs):
    keys, docs, out_ref = refs[:near], refs[near : 2 * near], refs[2 * near]
    rows = r_ref.shape[0]
    own = q_ref.shape[0]
    eight = 2 * own
    tokens = keys[0].shape[1]
    scale = 1.0 / math.sqrt(DN + DR)
    meta = q_ref[:, H * (DN + DR) :].astype(jnp.float32)
    meta = jnp.concatenate([meta, meta], axis=0)
    q_doc = meta[:, 0:1]
    q_pos = meta[:, 1:2] * 256.0 + meta[:, 2:3]
    me = me_ref[0]
    scores = []
    for k in range(near):
        latent = keys[k][:R, :]
        rope = keys[k][R:, :]
        both = jnp.dot(a_ref[...], latent, preferred_element_type=jnp.float32)
        turn = jnp.dot(
            r_ref[...], jnp.concatenate([rope, rope], axis=0), preferred_element_type=jnp.float32
        )
        found = (both[:rows] + both[rows:] + turn) * scale
        place = lax.bitwise_xor(me, k) * tokens + iota((eight, tokens), 1)
        visible = (docs[k][...].astype(jnp.float32) == q_doc) & (place.astype(jnp.float32) <= q_pos)
        found = jnp.where(visible[None], found.reshape(rows // eight, eight, tokens), HIDDEN)
        scores.append(found.reshape(rows, tokens))
    best = scores[0]
    for found in scores[1:]:
        best = jnp.maximum(best, found)
    best = jnp.maximum(jnp.max(best, axis=1, keepdims=True), FLOOR)
    total = None
    mixed = None
    for k in range(near):
        weights = jnp.exp(scores[k] - best)
        total = weights if total is None else total + weights
        high, low = split(weights)
        both = jnp.concatenate([high, low], axis=0).astype(jnp.bfloat16)
        part = lax.dot_general(
            both, keys[k][:R, :], (((1,), (1,)), ((), ())), preferred_element_type=jnp.float32
        )
        mixed = part if mixed is None else mixed + part
    total = jnp.sum(total, axis=1, keepdims=True)
    high, low = split(mixed[:rows] + mixed[rows:])
    lane = iota((eight, META), 1)
    stats = jnp.zeros((eight, META), jnp.float32)
    for pair in range(PAIRS):
        take = slice(pair * eight, (pair + 1) * eight)
        cols = slice(pair * 2 * DV, (pair + 1) * 2 * DV)
        lhs = jnp.concatenate([high[take], low[take]], axis=0).astype(jnp.bfloat16)
        res = jnp.dot(lhs, w_ref[:, cols], preferred_element_type=jnp.float32)
        res = res[:eight] + res[eight:]
        out_ref[:, cols] = jnp.concatenate([res[:own, :DV], res[own:, DV:]], axis=1)
        stats = jnp.where(lane == pair, best[take], stats)
        stats = jnp.where(lane == PAIRS + pair, total[take], stats)
    out_ref[:, H * DV : H * DV + META] = stats[:own]
    out_ref[:, H * DV + META :] = stats[own:]


def attend(me, absorbed, turned, query, w_uv, keys, docs):
    near = len(keys)
    return pl.pallas_call(
        functools.partial(attend_kernel, near),
        out_shape=jax.ShapeDtypeStruct((query.shape[0], H * DV + 2 * META), jnp.float32),
        in_specs=[SMEM] + [VMEM] * (4 + 2 * near),
        out_specs=VMEM,
        compiler_params=PARAMS,
        name="attend",
    )(me, absorbed, turned, query, w_uv, *keys, *docs)


def combine_kernel(count, *refs):
    parts, out_ref = refs[:count], refs[count]
    stats = [p[:, H * DV :] for p in parts]
    top = functools.reduce(jnp.maximum, stats)
    factors = [jnp.exp(s - top) for s in stats]
    total = None
    for s, f in zip(stats, factors):
        ends = [
            f[:, half * META : half * META + PAIRS]
            * s[:, half * META + PAIRS : half * META + 2 * PAIRS]
            for half in range(2)
        ]
        ends = jnp.concatenate(ends, axis=1)
        total = ends if total is None else total + ends
    for head in range(H):
        pair, half = head // 2, head % 2
        cols = slice(head * DV, (head + 1) * DV)
        lane = half * META + pair
        acc = None
        for p, f in zip(parts, factors):
            term = p[:, cols] * f[:, lane : lane + 1]
            acc = term if acc is None else acc + term
        lane = half * PAIRS + pair
        out_ref[:, cols] = (acc / total[:, lane : lane + 1]).astype(out_ref.dtype)


def combine(parts):
    return pl.pallas_call(
        functools.partial(combine_kernel, len(parts)),
        out_shape=jax.ShapeDtypeStruct((parts[0].shape[0], H * DV), jnp.bfloat16),
        in_specs=[VMEM] * len(parts),
        out_specs=VMEM,
        compiler_params=PARAMS,
        name="combine",
    )(*parts)


def shards(size, query_nope, query_rope, cache, key_docs, query_docs, query_pos, w_uk, w_uv):
    near = math.gcd(size, 4)
    far = size // near
    me = lax.axis_index("col")

    def swap(x, mask):
        return lax.ppermute(x, "col", [(i, i ^ mask) for i in range(size)])

    def gather(block):
        found = {0: block}
        if near == 4:
            found[2] = swap(block, 2)
        if near > 1:
            found[1] = swap(block, 1)
        if near == 4:
            found[3] = swap(found[2], 1)
        return [found[k] for k in range(near)]

    keys = gather(cache.T)
    docs = gather(key_docs.reshape(1, -1))

    meta = jnp.stack(
        [query_docs, lax.shift_right_logical(query_pos, 8), lax.bitwise_and(query_pos, 255)], axis=1
    ).astype(jnp.bfloat16)
    meta = jnp.pad(meta, ((0, 0), (0, META - 3)))
    mine = jnp.concatenate([query_nope, query_rope, meta], axis=1)
    groups = [mine] + [swap(mine, near * k) for k in range(1, far)]
    where = jnp.reshape(me, (1,)).astype(jnp.int32)
    parts = [None] * far
    for start in range(0, far, 4):
        some = groups[start : start + 4]
        absorbed, turned = absorb(some, w_uk)
        for g, query in enumerate(some):
            k = start + g
            part = attend(where, absorbed[g], turned[g], query, w_uv, keys, docs)
            parts[k] = part if k == 0 else swap(part, near * k)
    return combine(parts)


def solution(mesh):
    split_rows = P(("ga", "col"), None)
    split_flat = P(("ga", "col"))
    placed = (split_rows, split_rows, split_rows, split_flat, split_flat, split_flat, P(), P())
    size = mesh.shape["col"]

    def body(*arrays):
        return shards(size, *arrays)

    return jax.shard_map(body, mesh=mesh, in_specs=placed, out_specs=split_rows, check_vma=False)
```

```python
import functools
import math

import jax
import jax.numpy as jnp
from jax import lax
from jax.experimental import pallas as pl
from jax.experimental.pallas import tpu as pltpu
from jax.sharding import PartitionSpec as P


H = 32
DN = 128
DR = 64
DV = 128
R = 512
META = 128
PAIRS = H // 2
HIDDEN = -1e30
FLOOR = -1e29
VMEM = pl.BlockSpec(memory_space=pltpu.VMEM)
SMEM = pl.BlockSpec(memory_space=pltpu.SMEM)
PARAMS = pltpu.CompilerParams(vmem_limit_bytes=24 * 1024 * 1024)


def iota(shape, axis):
    return lax.broadcasted_iota(jnp.int32, shape, axis)


def split(x):
    high = x.astype(jnp.bfloat16).astype(jnp.float32)
    return high, x - high


def diagonal(x):
    wide = jnp.concatenate([x, x], axis=0)
    own, half = x.shape[0], x.shape[1] // 2
    keep = (iota(wide.shape, 0) // own) == (iota(wide.shape, 1) // half)
    return jnp.where(keep, wide, 0.0)


def touch_kernel(w_ref, out_ref):
    out_ref[...] = jnp.zeros_like(out_ref)


def touch(weights):
    return pl.pallas_call(
        touch_kernel,
        out_shape=jax.ShapeDtypeStruct((8, META), jnp.float32),
        in_specs=[VMEM],
        out_specs=VMEM,
        compiler_params=PARAMS,
        name="touch",
    )(weights)


def absorb_kernel(count, *refs):
    queries, (w_ref, _, a_ref, r_ref) = refs[:count], refs[count:]
    half = a_ref.shape[1] // 2
    step = 2 * half // PAIRS
    for duo in range(PAIRS // 2):
        found = []
        for pair in (2 * duo, 2 * duo + 1):
            cols = slice(pair * 2 * DN, (pair + 1) * 2 * DN)
            lhs = [diagonal(q[:, cols].astype(jnp.float32)) for q in queries]
            lhs = jnp.concatenate(lhs, axis=0).astype(jnp.bfloat16)
            found.append(
                lax.dot_general(
                    lhs, w_ref[:, cols], (((1,), (1,)), ((), ())), preferred_element_type=jnp.float32
                )
            )
        rows = slice(duo * step, (duo + 1) * step)
        low_rows = slice(half + duo * step, half + (duo + 1) * step)
        small = step // 2
        for g in range(count):
            own = slice(g * small, (g + 1) * small)
            high, low = split(jnp.concatenate([f[own] for f in found], axis=0))
            a_ref[g, rows] = high.astype(jnp.bfloat16)
            a_ref[g, low_rows] = low.astype(jnp.bfloat16)
            turned = []
            for pair in (2 * duo, 2 * duo + 1):
                cols = slice(H * DN + pair * 2 * DR, H * DN + (pair + 1) * 2 * DR)
                turned.append(diagonal(queries[g][:, cols].astype(jnp.float32)))
            r_ref[g, rows] = jnp.concatenate(turned, axis=0).astype(jnp.bfloat16)


def absorb(queries, w_uk, touched):
    count = len(queries)
    rows = queries[0].shape[0] * H
    return pl.pallas_call(
        functools.partial(absorb_kernel, count),
        out_shape=(
            jax.ShapeDtypeStruct((count, 2 * rows, R), jnp.bfloat16),
            jax.ShapeDtypeStruct((count, rows, 2 * DR), jnp.bfloat16),
        ),
        in_specs=[VMEM] * (count + 2),
        out_specs=(VMEM, VMEM),
        compiler_params=PARAMS,
        name="absorb",
    )(*queries, w_uk, touched)


def attend_kernel(near, me_ref, a_ref, r_ref, q_ref, w_ref, *refs):
    keys, docs, out_ref = refs[:near], refs[near:-1], refs[-1]
    rows = r_ref.shape[0]
    own = q_ref.shape[0]
    eight = 2 * own
    tokens = keys[0].shape[1]
    scale = 1.0 / math.sqrt(DN + DR)
    meta = q_ref[:, H * (DN + DR) :].astype(jnp.float32)
    pick = (iota((eight, META), 0) % own) == iota((eight, META), 1)
    meta = [jnp.sum(jnp.where(pick, meta[i : i + 1], 0.0), axis=1, keepdims=True) for i in range(3)]
    q_doc = meta[0]
    q_pos = meta[1] * 256.0 + meta[2]
    me = me_ref[0]
    scores = []
    for k in range(near):
        latent = keys[k][:R, :]
        rope = keys[k][R:, :]
        both = jnp.dot(a_ref[...], latent, preferred_element_type=jnp.float32)
        turn = jnp.dot(
            r_ref[...], jnp.concatenate([rope, rope], axis=0), preferred_element_type=jnp.float32
        )
        found = (both[:rows] + both[rows:] + turn) * scale
        place = lax.bitwise_xor(me, k) * tokens + iota((eight, tokens), 1)
        doc = docs[k // 2][:, (k % 2) * tokens : (k % 2 + 1) * tokens]
        visible = (doc.astype(jnp.float32) == q_doc) & (place.astype(jnp.float32) <= q_pos)
        found = jnp.where(visible[None], found.reshape(rows // eight, eight, tokens), HIDDEN)
        scores.append(found.reshape(rows, tokens))
    best = scores[0]
    for found in scores[1:]:
        best = jnp.maximum(best, found)
    best = jnp.maximum(jnp.max(best, axis=1, keepdims=True), FLOOR)
    total = None
    mixed = None
    for k in range(near):
        weights = jnp.exp(scores[k] - best)
        total = weights if total is None else total + weights
        high, low = split(weights)
        both = jnp.concatenate([high, low], axis=0).astype(jnp.bfloat16)
        part = lax.dot_general(
            both, keys[k][:R, :], (((1,), (1,)), ((), ())), preferred_element_type=jnp.float32
        )
        mixed = part if mixed is None else mixed + part
    total = jnp.sum(total, axis=1, keepdims=True)
    high, low = split(mixed[:rows] + mixed[rows:])
    lane = iota((eight, META), 1)
    stats = jnp.zeros((eight, META), jnp.float32)
    for pair in range(PAIRS):
        take = slice(pair * eight, (pair + 1) * eight)
        cols = slice(pair * 2 * DV, (pair + 1) * 2 * DV)
        lhs = jnp.concatenate([high[take], low[take]], axis=0).astype(jnp.bfloat16)
        res = jnp.dot(lhs, w_ref[:, cols], preferred_element_type=jnp.float32)
        res = res[:eight] + res[eight:]
        out_ref[:, cols] = jnp.concatenate([res[:own, :DV], res[own:, DV:]], axis=1)
        stats = jnp.where(lane == pair, best[take], stats)
        stats = jnp.where(lane == PAIRS + pair, total[take], stats)
    out_ref[:, H * DV : H * DV + META] = stats[:own]
    out_ref[:, H * DV + META :] = stats[own:]


def attend(me, absorbed, turned, query, w_uv, keys, docs):
    near = len(keys)
    return pl.pallas_call(
        functools.partial(attend_kernel, near),
        out_shape=jax.ShapeDtypeStruct((query.shape[0], H * DV + 2 * META), jnp.float32),
        in_specs=[SMEM] + [VMEM] * (4 + near + len(docs)),
        out_specs=VMEM,
        compiler_params=PARAMS,
        name="attend",
    )(me, absorbed, turned, query, w_uv, *keys, *docs)


def combine_kernel(count, *refs):
    parts, out_ref = refs[:count], refs[count]
    stats = [p[:, H * DV :] for p in parts]
    top = functools.reduce(jnp.maximum, stats)
    factors = [jnp.exp(s - top) for s in stats]
    total = None
    for s, f in zip(stats, factors):
        ends = [
            f[:, half * META : half * META + PAIRS]
            * s[:, half * META + PAIRS : half * META + 2 * PAIRS]
            for half in range(2)
        ]
        ends = jnp.concatenate(ends, axis=1)
        total = ends if total is None else total + ends
    for head in range(H):
        pair, half = head // 2, head % 2
        cols = slice(head * DV, (head + 1) * DV)
        lane = half * META + pair
        acc = None
        for p, f in zip(parts, factors):
            term = p[:, cols] * f[:, lane : lane + 1]
            acc = term if acc is None else acc + term
        lane = half * PAIRS + pair
        out_ref[:, cols] = (acc / total[:, lane : lane + 1]).astype(out_ref.dtype)


def combine(parts):
    return pl.pallas_call(
        functools.partial(combine_kernel, len(parts)),
        out_shape=jax.ShapeDtypeStruct((parts[0].shape[0], H * DV), jnp.bfloat16),
        in_specs=[VMEM] * len(parts),
        out_specs=VMEM,
        compiler_params=PARAMS,
        name="combine",
    )(*parts)


def shards(size, query_nope, query_rope, cache, key_docs, query_docs, query_pos, w_uk, w_uv):
    near = math.gcd(size, 4)
    far = size // near
    me = lax.axis_index("col")

    def swap(x, mask):
        return lax.ppermute(x, "col", [(i, i ^ mask) for i in range(size)])

    block, doc = cache.T, key_docs.reshape(1, -1)
    keys, docs = {0: block}, [doc]
    if near == 4:
        keys[2] = swap(block, 2)
    if near > 1:
        keys[1] = swap(block, 1)
        docs = [jnp.concatenate([doc, swap(doc, 1)], axis=1)]
    own_rows = query_nope.shape[0]
    meta = [query_docs, lax.shift_right_logical(query_pos, 8), lax.bitwise_and(query_pos, 255)]
    meta = jnp.pad(jnp.stack(meta), ((0, own_rows - 3), (0, META - own_rows)))
    mine = jnp.concatenate([query_nope, query_rope, meta.astype(query_nope.dtype)], axis=1)
    touched = touch(w_uk)
    groups = [mine]
    for k in range(1, far):
        groups.append(swap(mine, near * k))
    if near == 4:
        docs.append(swap(docs[0], 2))
        keys[3] = swap(keys[2], 1)
    keys = [keys[k] for k in range(near)]
    where = jnp.reshape(me, (1,)).astype(jnp.int32)
    parts = [None] * far
    for start in range(0, far, 4):
        some = groups[start : start + 4]
        absorbed, turned = absorb(some, w_uk, touched)
        for g, query in enumerate(some):
            k = start + g
            part = attend(where, absorbed[g], turned[g], query, w_uv, keys, docs)
            parts[k] = part if k == 0 else swap(part, near * k)
    return combine(parts)


def solution(mesh):
    split_rows = P(("ga", "col"), None)
    split_flat = P(("ga", "col"))
    placed = (split_rows, split_rows, split_rows, split_flat, split_flat, split_flat, P(), P())
    size = mesh.shape["col"]

    def body(*arrays):
        return shards(size, *arrays)

    return jax.shard_map(body, mesh=mesh, in_specs=placed, out_specs=split_rows, check_vma=False)
```

```python
import functools
import math

import jax
import jax.numpy as jnp
from jax import lax
from jax.experimental import pallas as pl
from jax.experimental.pallas import tpu as pltpu
from jax.sharding import PartitionSpec as P


H = 32
DN = 128
DR = 64
DV = 128
R = 512
META = 128
PAIRS = H // 2
LEAD = 2000000000
HIDDEN = -1e30
FLOOR = -1e29
VMEM = pl.BlockSpec(memory_space=pltpu.VMEM)
SMEM = pl.BlockSpec(memory_space=pltpu.SMEM)
SMALL = pltpu.CompilerParams(vmem_limit_bytes=2 * 1024 * 1024)
PARAMS = pltpu.CompilerParams(vmem_limit_bytes=24 * 1024 * 1024)


def iota(shape, axis):
    return lax.broadcasted_iota(jnp.int32, shape, axis)


def split(x):
    high = x.astype(jnp.bfloat16).astype(jnp.float32)
    return high, x - high


def diagonal(x):
    wide = jnp.concatenate([x, x], axis=0)
    own, half = x.shape[0], x.shape[1] // 2
    keep = (iota(wide.shape, 0) // own) == (iota(wide.shape, 1) // half)
    return jnp.where(keep, wide, 0.0)


def lead_kernel(out_ref):
    out_ref[...] = jnp.zeros_like(out_ref)


def lead(flops):
    return pl.pallas_call(
        lead_kernel,
        out_shape=jax.ShapeDtypeStruct((8, META), jnp.float32),
        out_specs=VMEM,
        compiler_params=SMALL,
        cost_estimate=pl.CostEstimate(flops=flops, transcendentals=0, bytes_accessed=4096),
        name="lead",
    )()


def pack_kernel(lead_ref, doc_ref, pos_ref, nope_ref, rope_ref, out_ref):
    rows = out_ref.shape[0]
    pos = pos_ref[...]
    meta = [doc_ref[...], lax.shift_right_logical(pos, 8), lax.bitwise_and(pos, 255)]
    meta.append(jnp.zeros((1, META - 3 * rows), jnp.int32))
    meta = jnp.concatenate(meta, axis=1).astype(jnp.float32)
    out_ref[:, : H * DN] = nope_ref[...]
    out_ref[:, H * DN : H * (DN + DR)] = rope_ref[...]
    out_ref[:, H * (DN + DR) :] = jnp.broadcast_to(meta, (rows, META)).astype(out_ref.dtype)


def pack(first, query_docs, query_pos, query_nope, query_rope):
    rows = query_nope.shape[0]
    width = query_nope.shape[1] + query_rope.shape[1] + META
    return pl.pallas_call(
        pack_kernel,
        out_shape=jax.ShapeDtypeStruct((rows, width), query_nope.dtype),
        in_specs=[VMEM] * 5,
        out_specs=VMEM,
        compiler_params=SMALL,
        name="pack",
    )(first, query_docs.reshape(1, rows), query_pos.reshape(1, rows), query_nope, query_rope)


def join_kernel(a_ref, b_ref, out_ref):
    out_ref[...] = jnp.concatenate([a_ref[...], b_ref[...]], axis=1)


def join(a, b):
    return pl.pallas_call(
        join_kernel,
        out_shape=jax.ShapeDtypeStruct((1, a.shape[1] + b.shape[1]), a.dtype),
        in_specs=[VMEM] * 2,
        out_specs=VMEM,
        compiler_params=SMALL,
        name="join",
    )(a, b)


def absorb_kernel(count, *refs):
    queries, (w_ref, _, a_ref, r_ref) = refs[:count], refs[count:]
    half = a_ref.shape[1] // 2
    step = 2 * half // PAIRS
    for duo in range(PAIRS // 2):
        found = []
        for pair in (2 * duo, 2 * duo + 1):
            cols = slice(pair * 2 * DN, (pair + 1) * 2 * DN)
            lhs = [diagonal(q[:, cols].astype(jnp.float32)) for q in queries]
            lhs = jnp.concatenate(lhs, axis=0).astype(jnp.bfloat16)
            found.append(
                lax.dot_general(
                    lhs, w_ref[:, cols], (((1,), (1,)), ((), ())), preferred_element_type=jnp.float32
                )
            )
        rows = slice(duo * step, (duo + 1) * step)
        low_rows = slice(half + duo * step, half + (duo + 1) * step)
        small = step // 2
        for g in range(count):
            own = slice(g * small, (g + 1) * small)
            high, low = split(jnp.concatenate([f[own] for f in found], axis=0))
            a_ref[g, rows] = high.astype(jnp.bfloat16)
            a_ref[g, low_rows] = low.astype(jnp.bfloat16)
            turned = []
            for pair in (2 * duo, 2 * duo + 1):
                cols = slice(H * DN + pair * 2 * DR, H * DN + (pair + 1) * 2 * DR)
                turned.append(diagonal(queries[g][:, cols].astype(jnp.float32)))
            r_ref[g, rows] = jnp.concatenate(turned, axis=0).astype(jnp.bfloat16)


def absorb(queries, w_uk, started):
    count = len(queries)
    rows = queries[0].shape[0] * H
    return pl.pallas_call(
        functools.partial(absorb_kernel, count),
        out_shape=(
            jax.ShapeDtypeStruct((count, 2 * rows, R), jnp.bfloat16),
            jax.ShapeDtypeStruct((count, rows, 2 * DR), jnp.bfloat16),
        ),
        in_specs=[VMEM] * (count + 2),
        out_specs=(VMEM, VMEM),
        compiler_params=PARAMS,
        name="absorb",
    )(*queries, w_uk, started)


def attend_kernel(near, count, first, me_ref, a_ref, r_ref, w_ref, *refs):
    queries, keys = refs[:count], refs[count : count + near]
    docs, outs = refs[count + near : -count], refs[-count:]
    rows = r_ref.shape[1]
    own = queries[0].shape[0]
    eight = 2 * own
    tokens = keys[0].shape[1]
    scale = 1.0 / math.sqrt(DN + DR)
    me = me_ref[0]
    group = range(count)

    spot = iota((eight, META), 0) % own
    lane = iota((eight, META), 1)
    limits = []
    for q in queries:
        meta = q[:1, H * (DN + DR) :].astype(jnp.float32)
        values = [
            jnp.sum(jnp.where(lane == spot + i * own, meta, 0.0), axis=1, keepdims=True)
            for i in range(3)
        ]
        limits.append((values[0], values[1] * 256.0 + values[2]))

    absorbed = jnp.concatenate([a_ref[first + g] for g in group], axis=0)
    turned = jnp.concatenate([r_ref[first + g] for g in group], axis=0)
    scores = [[] for _ in group]
    for k in range(near):
        latent = keys[k][:R, :]
        rope = keys[k][R:, :]
        both = jnp.dot(absorbed, latent, preferred_element_type=jnp.float32)
        turn = jnp.dot(
            turned, jnp.concatenate([rope, rope], axis=0), preferred_element_type=jnp.float32
        )
        place = lax.bitwise_xor(me, k) * tokens + iota((eight, tokens), 1)
        doc = docs[k // 2][:, (k % 2) * tokens : (k % 2 + 1) * tokens].astype(jnp.float32)
        for g in group:
            q_doc, q_pos = limits[g]
            visible = (doc == q_doc) & (place.astype(jnp.float32) <= q_pos)
            top = 2 * g * rows
            found = both[top : top + rows] + both[top + rows : top + 2 * rows]
            found = (found + turn[g * rows : (g + 1) * rows]) * scale
            found = found.reshape(rows // eight, eight, tokens)
            scores[g].append(jnp.where(visible[None], found, HIDDEN).reshape(rows, tokens))
    bests, totals = [], []
    for g in group:
        best = functools.reduce(jnp.maximum, scores[g])
        bests.append(jnp.maximum(jnp.max(best, axis=1, keepdims=True), FLOOR))
    mixed = None
    sums = [None for _ in group]
    for k in range(near):
        both = []
        for g in group:
            weights = jnp.exp(scores[g][k] - bests[g])
            sums[g] = weights if sums[g] is None else sums[g] + weights
            both += split(weights)
        both = jnp.concatenate(both, axis=0).astype(jnp.bfloat16)
        part = lax.dot_general(
            both, keys[k][:R, :], (((1,), (1,)), ((), ())), preferred_element_type=jnp.float32
        )
        mixed = part if mixed is None else mixed + part
    totals = [jnp.sum(s, axis=1, keepdims=True) for s in sums]
    halves = []
    for g in group:
        top = 2 * g * rows
        halves += split(mixed[top : top + rows] + mixed[top + rows : top + 2 * rows])
    stats = [jnp.zeros((eight, META), jnp.float32) for _ in group]
    for pair in range(PAIRS):
        take = slice(pair * eight, (pair + 1) * eight)
        cols = slice(pair * 2 * DV, (pair + 1) * 2 * DV)
        lhs = jnp.concatenate([h[take] for h in halves], axis=0).astype(jnp.bfloat16)
        res = jnp.dot(lhs, w_ref[:, cols], preferred_element_type=jnp.float32)
        for g in group:
            top = 2 * g * eight
            part = res[top : top + eight] + res[top + eight : top + 2 * eight]
            outs[g][:, cols] = jnp.concatenate([part[:own, :DV], part[own:, DV:]], axis=1)
            for base, value in ((0, bests[g]), (2 * PAIRS, totals[g])):
                at = base + pair + jnp.where(iota((eight, META), 0) < own, 0, PAIRS)
                stats[g] = jnp.where(lane == at, value[take], stats[g])
    for g in group:
        outs[g][:, H * DV :] = stats[g][:own] + stats[g][own:]


def attend(me, first, absorbed, turned, queries, w_uv, keys, docs):
    near, count = len(keys), len(queries)
    part = jax.ShapeDtypeStruct((queries[0].shape[0], H * DV + META), jnp.float32)
    return pl.pallas_call(
        functools.partial(attend_kernel, near, count, first),
        out_shape=(part,) * count,
        in_specs=[SMEM] + [VMEM] * (3 + count + near + len(docs)),
        out_specs=(VMEM,) * count,
        compiler_params=PARAMS,
        name="attend",
    )(me, absorbed, turned, w_uv, *queries, *keys, *docs)


def combine_kernel(count, *refs):
    parts, out_ref = refs[:count], refs[count]
    stats = [p[:, H * DV :] for p in parts]
    maxima = [s[:, :H] for s in stats]
    top = functools.reduce(jnp.maximum, maxima)
    factors = [jnp.exp(m - top) for m in maxima]
    total = functools.reduce(jnp.add, [f * s[:, H : 2 * H] for f, s in zip(factors, stats)])
    factors = [f / total for f in factors]
    for head in range(H):
        cols = slice(head * DV, (head + 1) * DV)
        lane = (head % 2) * PAIRS + head // 2
        terms = [p[:, cols] * f[:, lane : lane + 1] for p, f in zip(parts, factors)]
        out_ref[:, cols] = functools.reduce(jnp.add, terms).astype(out_ref.dtype)


def combine(parts):
    return pl.pallas_call(
        functools.partial(combine_kernel, len(parts)),
        out_shape=jax.ShapeDtypeStruct((parts[0].shape[0], H * DV), jnp.bfloat16),
        in_specs=[VMEM] * len(parts),
        out_specs=VMEM,
        compiler_params=PARAMS,
        name="combine",
    )(*parts)


def shards(size, query_nope, query_rope, cache, key_docs, query_docs, query_pos, w_uk, w_uv):
    near = math.gcd(size, 4)
    far = size // near
    me = lax.axis_index("col")

    def swap(x, mask):
        return lax.ppermute(x, "col", [(i, i ^ mask) for i in range(size)])

    block, doc = cache.T, key_docs.reshape(1, -1)
    keys, docs = {0: block}, [doc]
    if near == 4:
        keys[2] = swap(block, 2)
    if near > 1:
        keys[1] = swap(block, 1)
        docs = [join(doc, swap(doc, 1))]
    first = lead(LEAD)
    mine = pack(first, query_docs, query_pos, query_nope, query_rope)
    groups = [mine]
    for k in range(1, far):
        groups.append(swap(mine, near * k))
    if near == 4:
        docs.append(swap(docs[0], 2))
        keys[3] = swap(keys[2], 1)
    keys = [keys[k] for k in range(near)]
    started = lead(4 * LEAD)
    where = jnp.reshape(me, (1,)).astype(jnp.int32)
    parts = [None] * far
    for start in range(0, far, 4):
        some = groups[start : start + 4]
        absorbed, turned = absorb(some, w_uk, started)
        for first in range(len(some) - len(some) % 2, -1, -2):
            pick = some[first : first + 2]
            if not pick:
                continue
            found = attend(where, first, absorbed, turned, pick, w_uv, keys, docs)
            for g, part in enumerate(found):
                k = start + first + g
                parts[k] = part if k == 0 else swap(part, near * k)
    return combine(parts)


def solution(mesh):
    split_rows = P(("ga", "col"), None)
    split_flat = P(("ga", "col"))
    placed = (split_rows, split_rows, split_rows, split_flat, split_flat, split_flat, P(), P())
    size = mesh.shape["col"]

    def body(*arrays):
        return shards(size, *arrays)

    return jax.shard_map(body, mesh=mesh, in_specs=placed, out_specs=split_rows, check_vma=False)
```

```python
import functools
import math

import jax
import jax.numpy as jnp
from jax import lax
from jax.experimental import pallas as pl
from jax.experimental.pallas import tpu as pltpu
from jax.sharding import PartitionSpec as P


H = 32
DN = 128
DR = 64
DV = 128
R = 512
META = 128
PAIRS = H // 2
LEAD = 2000000000
HIDDEN = -1e30
FLOOR = -1e29
VMEM = pl.BlockSpec(memory_space=pltpu.VMEM)
SMEM = pl.BlockSpec(memory_space=pltpu.SMEM)
SMALL = pltpu.CompilerParams(vmem_limit_bytes=2 * 1024 * 1024)
PARAMS = pltpu.CompilerParams(vmem_limit_bytes=24 * 1024 * 1024)


def iota(shape, axis):
    return lax.broadcasted_iota(jnp.int32, shape, axis)


def split(x):
    high = x.astype(jnp.bfloat16).astype(jnp.float32)
    return high, x - high


def diagonal(x):
    wide = jnp.concatenate([x, x], axis=0)
    own, half = x.shape[0], x.shape[1] // 2
    keep = (iota(wide.shape, 0) // own) == (iota(wide.shape, 1) // half)
    return jnp.where(keep, wide, 0.0)


def lead_kernel(out_ref):
    out_ref[...] = jnp.zeros_like(out_ref)


def lead(flops):
    return pl.pallas_call(
        lead_kernel,
        out_shape=jax.ShapeDtypeStruct((8, META), jnp.float32),
        out_specs=VMEM,
        compiler_params=SMALL,
        cost_estimate=pl.CostEstimate(flops=flops, transcendentals=0, bytes_accessed=4096),
        name="lead",
    )()


def pack_kernel(lead_ref, doc_ref, pos_ref, nope_ref, rope_ref, out_ref):
    rows = out_ref.shape[0]
    pos = pos_ref[...]
    meta = [doc_ref[...], lax.shift_right_logical(pos, 8), lax.bitwise_and(pos, 255)]
    meta.append(jnp.zeros((1, META - 3 * rows), jnp.int32))
    meta = jnp.concatenate(meta, axis=1).astype(jnp.float32)
    out_ref[:, : H * DN] = nope_ref[...]
    out_ref[:, H * DN : H * (DN + DR)] = rope_ref[...]
    out_ref[:, H * (DN + DR) :] = jnp.broadcast_to(meta, (rows, META)).astype(out_ref.dtype)


def pack(first, query_docs, query_pos, query_nope, query_rope):
    rows = query_nope.shape[0]
    width = query_nope.shape[1] + query_rope.shape[1] + META
    return pl.pallas_call(
        pack_kernel,
        out_shape=jax.ShapeDtypeStruct((rows, width), query_nope.dtype),
        in_specs=[VMEM] * 5,
        out_specs=VMEM,
        compiler_params=SMALL,
        name="pack",
    )(first, query_docs.reshape(1, rows), query_pos.reshape(1, rows), query_nope, query_rope)


def join_kernel(a_ref, b_ref, out_ref):
    out_ref[...] = jnp.concatenate([a_ref[...], b_ref[...]], axis=1)


def join(a, b):
    return pl.pallas_call(
        join_kernel,
        out_shape=jax.ShapeDtypeStruct((1, a.shape[1] + b.shape[1]), a.dtype),
        in_specs=[VMEM] * 2,
        out_specs=VMEM,
        compiler_params=SMALL,
        name="join",
    )(a, b)


def absorb_kernel(count, *refs):
    queries, (w_ref, _, a_ref, r_ref) = refs[:count], refs[count:]
    half = a_ref.shape[1] // 2
    step = 2 * half // PAIRS
    for duo in range(PAIRS // 2):
        found = []
        for pair in (2 * duo, 2 * duo + 1):
            cols = slice(pair * 2 * DN, (pair + 1) * 2 * DN)
            lhs = [diagonal(q[:, cols].astype(jnp.float32)) for q in queries]
            lhs = jnp.concatenate(lhs, axis=0).astype(jnp.bfloat16)
            found.append(
                lax.dot_general(
                    lhs, w_ref[:, cols], (((1,), (1,)), ((), ())), preferred_element_type=jnp.float32
                )
            )
        rows = slice(duo * step, (duo + 1) * step)
        low_rows = slice(half + duo * step, half + (duo + 1) * step)
        small = step // 2
        for g in range(count):
            own = slice(g * small, (g + 1) * small)
            high, low = split(jnp.concatenate([f[own] for f in found], axis=0))
            a_ref[g, rows] = high.astype(jnp.bfloat16)
            a_ref[g, low_rows] = low.astype(jnp.bfloat16)
            turned = []
            for pair in (2 * duo, 2 * duo + 1):
                cols = slice(H * DN + pair * 2 * DR, H * DN + (pair + 1) * 2 * DR)
                turned.append(diagonal(queries[g][:, cols].astype(jnp.float32)))
            r_ref[g, rows] = jnp.concatenate(turned, axis=0).astype(jnp.bfloat16)


def absorb(queries, w_uk, started):
    count = len(queries)
    rows = queries[0].shape[0] * H
    return pl.pallas_call(
        functools.partial(absorb_kernel, count),
        out_shape=(
            jax.ShapeDtypeStruct((count, 2 * rows, R), jnp.bfloat16),
            jax.ShapeDtypeStruct((count, rows, 2 * DR), jnp.bfloat16),
        ),
        in_specs=[VMEM] * (count + 2),
        out_specs=(VMEM, VMEM),
        compiler_params=PARAMS,
        name="absorb",
    )(*queries, w_uk, started)


def attend_kernel(near, count, first, me_ref, a_ref, r_ref, w_ref, *refs):
    queries, keys = refs[:count], refs[count : count + near]
    docs, outs = refs[count + near : -count], refs[-count:]
    rows = r_ref.shape[1]
    own = queries[0].shape[0]
    eight = 2 * own
    tokens = keys[0].shape[1]
    scale = 1.0 / math.sqrt(DN + DR)
    me = me_ref[0]
    group = range(count)

    spot = iota((eight, META), 0) % own
    lane = iota((eight, META), 1)
    limits = []
    for q in queries:
        meta = q[:1, H * (DN + DR) :].astype(jnp.float32)
        values = [
            jnp.sum(jnp.where(lane == spot + i * own, meta, 0.0), axis=1, keepdims=True)
            for i in range(3)
        ]
        limits.append((values[0], values[1] * 256.0 + values[2]))

    absorbed = jnp.concatenate([a_ref[first + g] for g in group], axis=0)
    turned = jnp.concatenate([r_ref[first + g] for g in group], axis=0)
    scores = [[] for _ in group]
    for k in range(near):
        latent = keys[k][:R, :]
        rope = keys[k][R:, :]
        both = jnp.dot(absorbed, latent, preferred_element_type=jnp.float32)
        turn = jnp.dot(
            turned, jnp.concatenate([rope, rope], axis=0), preferred_element_type=jnp.float32
        )
        place = lax.bitwise_xor(me, k) * tokens + iota((eight, tokens), 1)
        doc = docs[k // 2][:, (k % 2) * tokens : (k % 2 + 1) * tokens].astype(jnp.float32)
        for g in group:
            q_doc, q_pos = limits[g]
            visible = (doc == q_doc) & (place.astype(jnp.float32) <= q_pos)
            top = 2 * g * rows
            found = both[top : top + rows] + both[top + rows : top + 2 * rows]
            found = (found + turn[g * rows : (g + 1) * rows]) * scale
            found = found.reshape(rows // eight, eight, tokens)
            scores[g].append(jnp.where(visible[None], found, HIDDEN).reshape(rows, tokens))
    bests, totals = [], []
    for g in group:
        best = functools.reduce(jnp.maximum, scores[g])
        bests.append(jnp.maximum(jnp.max(best, axis=1, keepdims=True), FLOOR))
    mixed = None
    sums = [None for _ in group]
    for k in range(near):
        both = []
        for g in group:
            weights = jnp.exp(scores[g][k] - bests[g])
            sums[g] = weights if sums[g] is None else sums[g] + weights
            both += split(weights)
        both = jnp.concatenate(both, axis=0).astype(jnp.bfloat16)
        part = lax.dot_general(
            both, keys[k][:R, :], (((1,), (1,)), ((), ())), preferred_element_type=jnp.float32
        )
        mixed = part if mixed is None else mixed + part
    totals = [jnp.sum(s, axis=1, keepdims=True) for s in sums]
    halves = []
    for g in group:
        top = 2 * g * rows
        halves += split(mixed[top : top + rows] + mixed[top + rows : top + 2 * rows])
    stats = [jnp.zeros((eight, META), jnp.float32) for _ in group]
    for pair in range(PAIRS):
        take = slice(pair * eight, (pair + 1) * eight)
        cols = slice(pair * 2 * DV, (pair + 1) * 2 * DV)
        lhs = jnp.concatenate([h[take] for h in halves], axis=0).astype(jnp.bfloat16)
        res = jnp.dot(lhs, w_ref[:, cols], preferred_element_type=jnp.float32)
        for g in group:
            top = 2 * g * eight
            part = res[top : top + eight] + res[top + eight : top + 2 * eight]
            outs[g][:, cols] = jnp.concatenate([part[:own, :DV], part[own:, DV:]], axis=1)
            for base, value in ((0, bests[g]), (2 * PAIRS, totals[g])):
                at = base + pair + jnp.where(iota((eight, META), 0) < own, 0, PAIRS)
                stats[g] = jnp.where(lane == at, value[take], stats[g])
    for g in group:
        outs[g][:, H * DV :] = stats[g][:own] + stats[g][own:]


def attend(me, first, absorbed, turned, queries, w_uv, keys, docs):
    near, count = len(keys), len(queries)
    part = jax.ShapeDtypeStruct((queries[0].shape[0], H * DV + META), jnp.float32)
    return pl.pallas_call(
        functools.partial(attend_kernel, near, count, first),
        out_shape=(part,) * count,
        in_specs=[SMEM] + [VMEM] * (3 + count + near + len(docs)),
        out_specs=(VMEM,) * count,
        compiler_params=PARAMS,
        name="attend",
    )(me, absorbed, turned, w_uv, *queries, *keys, *docs)


def combine_kernel(count, *refs):
    parts, out_ref = refs[:count], refs[count]
    stats = [p[:, H * DV :] for p in parts]
    maxima = [s[:, :H] for s in stats]
    top = functools.reduce(jnp.maximum, maxima)
    factors = [jnp.exp(m - top) for m in maxima]
    total = functools.reduce(jnp.add, [f * s[:, H : 2 * H] for f, s in zip(factors, stats)])
    factors = [f / total for f in factors]
    for head in range(H):
        cols = slice(head * DV, (head + 1) * DV)
        lane = (head % 2) * PAIRS + head // 2
        terms = [p[:, cols] * f[:, lane : lane + 1] for p, f in zip(parts, factors)]
        out_ref[:, cols] = functools.reduce(jnp.add, terms).astype(out_ref.dtype)


def combine(parts):
    return pl.pallas_call(
        functools.partial(combine_kernel, len(parts)),
        out_shape=jax.ShapeDtypeStruct((parts[0].shape[0], H * DV), jnp.bfloat16),
        in_specs=[VMEM] * len(parts),
        out_specs=VMEM,
        compiler_params=PARAMS,
        name="combine",
    )(*parts)


def shards(size, query_nope, query_rope, cache, key_docs, query_docs, query_pos, w_uk, w_uv):
    near = math.gcd(size, 4)
    far = size // near
    me = lax.axis_index("col")

    def swap(x, mask):
        return lax.ppermute(x, "col", [(i, i ^ mask) for i in range(size)])

    block, doc = cache.T, key_docs.reshape(1, -1)
    keys, docs = {0: block}, [doc]
    if near == 4:
        keys[2] = swap(block, 2)
    if near > 1:
        keys[1] = swap(block, 1)
        docs = [join(doc, swap(doc, 1))]
    first = lead(LEAD)
    mine = pack(first, query_docs, query_pos, query_nope, query_rope)
    groups = [mine]
    for k in range(1, far):
        groups.append(swap(mine, near * k))
    if near == 4:
        docs.append(swap(docs[0], 2))
        keys[3] = swap(keys[2], 1)
    keys = [keys[k] for k in range(near)]
    started = lead(4 * LEAD)
    where = jnp.reshape(me, (1,)).astype(jnp.int32)
    parts = [None] * far
    for start in range(0, far, 4):
        some = groups[start : start + 4]
        absorbed, turned = absorb(some, w_uk, started)
        cuts = [(1, len(some)), (0, 1)] if start == 0 else [(0, len(some))]
        for first, end in cuts:
            if first >= end:
                continue
            pick = some[first:end]
            found = attend(where, first, absorbed, turned, pick, w_uv, keys, docs)
            for g, part in enumerate(found):
                k = start + first + g
                parts[k] = part if k == 0 else swap(part, near * k)
    return combine(parts)


def solution(mesh):
    split_rows = P(("ga", "col"), None)
    split_flat = P(("ga", "col"))
    placed = (split_rows, split_rows, split_rows, split_flat, split_flat, split_flat, P(), P())
    size = mesh.shape["col"]

    def body(*arrays):
        return shards(size, *arrays)

    return jax.shard_map(body, mesh=mesh, in_specs=placed, out_specs=split_rows, check_vma=False)
```

```python
import functools
import math

import jax
import jax.numpy as jnp
from jax import lax
from jax.experimental import pallas as pl
from jax.experimental.pallas import tpu as pltpu
from jax.sharding import PartitionSpec as P


H = 32
DN = 128
DR = 64
DV = 128
R = 512
META = 128
PAIRS = H // 2
LEAD = 2000000000
HIDDEN = -1e30
FLOOR = -1e29
VMEM = pl.BlockSpec(memory_space=pltpu.VMEM)
SMEM = pl.BlockSpec(memory_space=pltpu.SMEM)
SMALL = pltpu.CompilerParams(vmem_limit_bytes=2 * 1024 * 1024)
PARAMS = pltpu.CompilerParams(vmem_limit_bytes=24 * 1024 * 1024)


def iota(shape, axis):
    return lax.broadcasted_iota(jnp.int32, shape, axis)


def split(x):
    high = x.astype(jnp.bfloat16).astype(jnp.float32)
    return high, x - high


def diagonal(x):
    wide = jnp.concatenate([x, x], axis=0)
    own, half = x.shape[0], x.shape[1] // 2
    keep = (iota(wide.shape, 0) // own) == (iota(wide.shape, 1) // half)
    return jnp.where(keep, wide, 0.0)


def lead_kernel(out_ref):
    out_ref[...] = jnp.zeros_like(out_ref)


def lead(flops):
    return pl.pallas_call(
        lead_kernel,
        out_shape=jax.ShapeDtypeStruct((8, META), jnp.float32),
        out_specs=VMEM,
        compiler_params=SMALL,
        cost_estimate=pl.CostEstimate(flops=flops, transcendentals=0, bytes_accessed=4096),
        name="lead",
    )()


def pack_kernel(lead_ref, doc_ref, pos_ref, nope_ref, rope_ref, out_ref):
    rows = out_ref.shape[0]
    pos = pos_ref[...]
    meta = [doc_ref[...], lax.shift_right_logical(pos, 8), lax.bitwise_and(pos, 255)]
    meta.append(jnp.zeros((1, META - 3 * rows), jnp.int32))
    meta = jnp.concatenate(meta, axis=1).astype(jnp.float32)
    out_ref[:, : H * DN] = nope_ref[...]
    out_ref[:, H * DN : H * (DN + DR)] = rope_ref[...]
    out_ref[:, H * (DN + DR) :] = jnp.broadcast_to(meta, (rows, META)).astype(out_ref.dtype)


def pack(first, query_docs, query_pos, query_nope, query_rope):
    rows = query_nope.shape[0]
    width = query_nope.shape[1] + query_rope.shape[1] + META
    return pl.pallas_call(
        pack_kernel,
        out_shape=jax.ShapeDtypeStruct((rows, width), query_nope.dtype),
        in_specs=[VMEM] * 5,
        out_specs=VMEM,
        compiler_params=SMALL,
        name="pack",
    )(first, query_docs.reshape(1, rows), query_pos.reshape(1, rows), query_nope, query_rope)


def join_kernel(a_ref, b_ref, out_ref):
    out_ref[...] = jnp.concatenate([a_ref[...], b_ref[...]], axis=1)


def join(a, b):
    return pl.pallas_call(
        join_kernel,
        out_shape=jax.ShapeDtypeStruct((1, a.shape[1] + b.shape[1]), a.dtype),
        in_specs=[VMEM] * 2,
        out_specs=VMEM,
        compiler_params=SMALL,
        name="join",
    )(a, b)


def absorb_kernel(count, *refs):
    queries, (w_ref, _, a_ref, r_ref) = refs[:count], refs[count:]
    half = a_ref.shape[1] // 2
    step = 2 * half // PAIRS
    for duo in range(PAIRS // 2):
        found = []
        for pair in (2 * duo, 2 * duo + 1):
            cols = slice(pair * 2 * DN, (pair + 1) * 2 * DN)
            lhs = [diagonal(q[:, cols].astype(jnp.float32)) for q in queries]
            lhs = jnp.concatenate(lhs, axis=0).astype(jnp.bfloat16)
            found.append(
                lax.dot_general(
                    lhs, w_ref[:, cols], (((1,), (1,)), ((), ())), preferred_element_type=jnp.float32
                )
            )
        rows = slice(duo * step, (duo + 1) * step)
        low_rows = slice(half + duo * step, half + (duo + 1) * step)
        small = step // 2
        for g in range(count):
            own = slice(g * small, (g + 1) * small)
            high, low = split(jnp.concatenate([f[own] for f in found], axis=0))
            a_ref[g, rows] = high.astype(jnp.bfloat16)
            a_ref[g, low_rows] = low.astype(jnp.bfloat16)
            turned = []
            for pair in (2 * duo, 2 * duo + 1):
                cols = slice(H * DN + pair * 2 * DR, H * DN + (pair + 1) * 2 * DR)
                turned.append(diagonal(queries[g][:, cols].astype(jnp.float32)))
            r_ref[g, rows] = jnp.concatenate(turned, axis=0).astype(jnp.bfloat16)


def absorb(queries, w_uk, started):
    count = len(queries)
    rows = queries[0].shape[0] * H
    return pl.pallas_call(
        functools.partial(absorb_kernel, count),
        out_shape=(
            jax.ShapeDtypeStruct((count, 2 * rows, R), jnp.bfloat16),
            jax.ShapeDtypeStruct((count, rows, 2 * DR), jnp.bfloat16),
        ),
        in_specs=[VMEM] * (count + 2),
        out_specs=(VMEM, VMEM),
        compiler_params=PARAMS,
        name="absorb",
    )(*queries, w_uk, started)


def attend_kernel(near, count, first, me_ref, a_ref, r_ref, w_ref, *refs):
    queries, keys = refs[:count], refs[count : count + near]
    docs, outs = refs[count + near : -count], refs[-count:]
    rows = r_ref.shape[1]
    own = queries[0].shape[0]
    eight = 2 * own
    tokens = keys[0].shape[1]
    scale = 1.0 / math.sqrt(DN + DR)
    me = me_ref[0]
    group = range(count)

    spot = iota((eight, META), 0) % own
    lane = iota((eight, META), 1)
    limits = []
    for q in queries:
        meta = q[:1, H * (DN + DR) :].astype(jnp.float32)
        values = [
            jnp.sum(jnp.where(lane == spot + i * own, meta, 0.0), axis=1, keepdims=True)
            for i in range(3)
        ]
        limits.append((values[0], values[1] * 256.0 + values[2]))

    absorbed = jnp.concatenate([a_ref[first + g] for g in group], axis=0)
    turned = jnp.concatenate([r_ref[first + g] for g in group], axis=0)
    scores = [[] for _ in group]
    for k in range(near):
        latent = keys[k][:R, :]
        rope = keys[k][R:, :]
        both = jnp.dot(absorbed, latent, preferred_element_type=jnp.float32)
        turn = jnp.dot(
            turned, jnp.concatenate([rope, rope], axis=0), preferred_element_type=jnp.float32
        )
        place = lax.bitwise_xor(me, k) * tokens + iota((eight, tokens), 1)
        doc = docs[k // 2][:, (k % 2) * tokens : (k % 2 + 1) * tokens].astype(jnp.float32)
        for g in group:
            q_doc, q_pos = limits[g]
            visible = (doc == q_doc) & (place.astype(jnp.float32) <= q_pos)
            top = 2 * g * rows
            found = both[top : top + rows] + both[top + rows : top + 2 * rows]
            found = (found + turn[g * rows : (g + 1) * rows]) * scale
            found = found.reshape(rows // eight, eight, tokens)
            scores[g].append(jnp.where(visible[None], found, HIDDEN).reshape(rows, tokens))
    bests, totals = [], []
    for g in group:
        best = functools.reduce(jnp.maximum, scores[g])
        bests.append(jnp.maximum(jnp.max(best, axis=1, keepdims=True), FLOOR))
    mixed = None
    sums = [None for _ in group]
    for k in range(near):
        both = []
        for g in group:
            weights = jnp.exp(scores[g][k] - bests[g])
            sums[g] = weights if sums[g] is None else sums[g] + weights
            both += split(weights)
        both = jnp.concatenate(both, axis=0).astype(jnp.bfloat16)
        part = lax.dot_general(
            both, keys[k][:R, :], (((1,), (1,)), ((), ())), preferred_element_type=jnp.float32
        )
        mixed = part if mixed is None else mixed + part
    totals = [jnp.sum(s, axis=1, keepdims=True) for s in sums]
    halves = []
    for g in group:
        top = 2 * g * rows
        halves += split(mixed[top : top + rows] + mixed[top + rows : top + 2 * rows])
    stats = [jnp.zeros((eight, META), jnp.float32) for _ in group]
    for pair in range(PAIRS):
        take = slice(pair * eight, (pair + 1) * eight)
        cols = slice(pair * 2 * DV, (pair + 1) * 2 * DV)
        lhs = jnp.concatenate([h[take] for h in halves], axis=0).astype(jnp.bfloat16)
        res = jnp.dot(lhs, w_ref[:, cols], preferred_element_type=jnp.float32)
        for g in group:
            top = 2 * g * eight
            part = res[top : top + eight] + res[top + eight : top + 2 * eight]
            outs[g][:, cols] = jnp.concatenate([part[:own, :DV], part[own:, DV:]], axis=1)
            for base, value in ((0, bests[g]), (2 * PAIRS, totals[g])):
                at = base + pair + jnp.where(iota((eight, META), 0) < own, 0, PAIRS)
                stats[g] = jnp.where(lane == at, value[take], stats[g])
    for g in group:
        outs[g][:, H * DV :] = stats[g][:own] + stats[g][own:]


def attend(me, first, absorbed, turned, queries, w_uv, keys, docs):
    near, count = len(keys), len(queries)
    part = jax.ShapeDtypeStruct((queries[0].shape[0], H * DV + META), jnp.float32)
    return pl.pallas_call(
        functools.partial(attend_kernel, near, count, first),
        out_shape=(part,) * count,
        in_specs=[SMEM] + [VMEM] * (3 + count + near + len(docs)),
        out_specs=(VMEM,) * count,
        compiler_params=PARAMS,
        name="attend",
    )(me, absorbed, turned, w_uv, *queries, *keys, *docs)


def weigh(parts):
    stats = [p[:, H * DV :] for p in parts]
    maxima = [s[:, :H] for s in stats]
    top = functools.reduce(jnp.maximum, maxima)
    factors = [jnp.exp(m - top) for m in maxima]
    total = functools.reduce(jnp.add, [f * s[:, H : 2 * H] for f, s in zip(factors, stats)])
    return top, factors, total


def blend(parts, factors, head):
    lane = (head % 2) * PAIRS + head // 2
    cols = slice(head * DV, (head + 1) * DV)
    return functools.reduce(
        jnp.add, [p[:, cols] * f[:, lane : lane + 1] for p, f in zip(parts, factors)]
    )


def merge_kernel(count, *refs):
    parts, out_ref = refs[:count], refs[count]
    top, factors, total = weigh(parts)
    for head in range(H):
        out_ref[:, head * DV : (head + 1) * DV] = blend(parts, factors, head)
    rest = jnp.zeros((out_ref.shape[0], META - 2 * H), jnp.float32)
    out_ref[:, H * DV :] = jnp.concatenate([top, total, rest], axis=1)


def merge(parts):
    return pl.pallas_call(
        functools.partial(merge_kernel, len(parts)),
        out_shape=jax.ShapeDtypeStruct(parts[0].shape, jnp.float32),
        in_specs=[VMEM] * len(parts),
        out_specs=VMEM,
        compiler_params=PARAMS,
        name="merge",
    )(*parts)


def combine_kernel(count, *refs):
    parts, out_ref = refs[:count], refs[count]
    _, factors, total = weigh(parts)
    factors = [f / total for f in factors]
    for head in range(H):
        value = blend(parts, factors, head)
        out_ref[:, head * DV : (head + 1) * DV] = value.astype(out_ref.dtype)


def combine(parts):
    return pl.pallas_call(
        functools.partial(combine_kernel, len(parts)),
        out_shape=jax.ShapeDtypeStruct((parts[0].shape[0], H * DV), jnp.bfloat16),
        in_specs=[VMEM] * len(parts),
        out_specs=VMEM,
        compiler_params=PARAMS,
        name="combine",
    )(*parts)


def shards(size, query_nope, query_rope, cache, key_docs, query_docs, query_pos, w_uk, w_uv):
    near = math.gcd(size, 4)
    far = size // near
    me = lax.axis_index("col")

    def swap(x, mask):
        return lax.ppermute(x, "col", [(i, i ^ mask) for i in range(size)])

    block, doc = cache.T, key_docs.reshape(1, -1)
    keys, docs = {0: block}, [doc]
    if near == 4:
        keys[2] = swap(block, 2)
    if near > 1:
        keys[1] = swap(block, 1)
        docs = [join(doc, swap(doc, 1))]
    first = lead(LEAD)
    mine = pack(first, query_docs, query_pos, query_nope, query_rope)
    groups = [mine]
    for k in range(1, far):
        groups.append(swap(mine, near * k))
    if near == 4:
        docs.append(swap(docs[0], 2))
        keys[3] = swap(keys[2], 1)
    keys = [keys[k] for k in range(near)]
    started = lead(4 * LEAD)
    where = jnp.reshape(me, (1,)).astype(jnp.int32)
    parts = [None] * far
    for start in range(0, far, 4):
        some = groups[start : start + 4]
        absorbed, turned = absorb(some, w_uk, started)
        cuts = [(2, len(some)), (1, 2), (0, 1)] if start == 0 else [(0, len(some))]
        for first, end in cuts:
            if first >= end:
                continue
            pick = some[first:end]
            found = attend(where, first, absorbed, turned, pick, w_uv, keys, docs)
            for g, part in enumerate(found):
                k = start + first + g
                parts[k] = part if k == 0 else swap(part, near * k)
    if far > 2:
        parts = [merge(parts[:1] + parts[2:]), parts[1]]
    return combine(parts)


def solution(mesh):
    split_rows = P(("ga", "col"), None)
    split_flat = P(("ga", "col"))
    placed = (split_rows, split_rows, split_rows, split_flat, split_flat, split_flat, P(), P())
    size = mesh.shape["col"]

    def body(*arrays):
        return shards(size, *arrays)

    return jax.shard_map(body, mesh=mesh, in_specs=placed, out_specs=split_rows, check_vma=False)
```

```python
import functools
import math

import jax
import jax.numpy as jnp
from jax import lax
from jax.experimental import pallas as pl
from jax.experimental.pallas import tpu as pltpu
from jax.sharding import PartitionSpec as P


H = 32
DN = 128
DR = 64
DV = 128
R = 512
META = 128
PAIRS = H // 2
LEAD = 2000000000
HIDDEN = -1e30
FLOOR = -1e29
VMEM = pl.BlockSpec(memory_space=pltpu.VMEM)
SMEM = pl.BlockSpec(memory_space=pltpu.SMEM)
SMALL = pltpu.CompilerParams(vmem_limit_bytes=2 * 1024 * 1024)
PARAMS = pltpu.CompilerParams(vmem_limit_bytes=24 * 1024 * 1024)


def iota(shape, axis):
    return lax.broadcasted_iota(jnp.int32, shape, axis)


def split(x):
    high = x.astype(jnp.bfloat16).astype(jnp.float32)
    return high, x - high


def diagonal(x):
    wide = jnp.concatenate([x, x], axis=0)
    own, half = x.shape[0], x.shape[1] // 2
    keep = (iota(wide.shape, 0) // own) == (iota(wide.shape, 1) // half)
    return jnp.where(keep, wide, 0.0)


def lead_kernel(out_ref):
    out_ref[...] = jnp.zeros_like(out_ref)


def lead(flops):
    return pl.pallas_call(
        lead_kernel,
        out_shape=jax.ShapeDtypeStruct((8, META), jnp.float32),
        out_specs=VMEM,
        compiler_params=SMALL,
        cost_estimate=pl.CostEstimate(flops=flops, transcendentals=0, bytes_accessed=4096),
        name="lead",
    )()


def pack_kernel(lead_ref, doc_ref, pos_ref, nope_ref, rope_ref, out_ref):
    rows = out_ref.shape[0]
    pos = pos_ref[...]
    meta = [doc_ref[...], lax.shift_right_logical(pos, 8), lax.bitwise_and(pos, 255)]
    meta.append(jnp.zeros((1, META - 3 * rows), jnp.int32))
    meta = jnp.concatenate(meta, axis=1).astype(jnp.float32)
    out_ref[:, : H * DN] = nope_ref[...]
    out_ref[:, H * DN : H * (DN + DR)] = rope_ref[...]
    out_ref[:, H * (DN + DR) :] = jnp.broadcast_to(meta, (rows, META)).astype(out_ref.dtype)


def pack(first, query_docs, query_pos, query_nope, query_rope):
    rows = query_nope.shape[0]
    width = query_nope.shape[1] + query_rope.shape[1] + META
    return pl.pallas_call(
        pack_kernel,
        out_shape=jax.ShapeDtypeStruct((rows, width), query_nope.dtype),
        in_specs=[VMEM] * 5,
        out_specs=VMEM,
        compiler_params=SMALL,
        name="pack",
    )(first, query_docs.reshape(1, rows), query_pos.reshape(1, rows), query_nope, query_rope)


def join_kernel(a_ref, b_ref, out_ref):
    out_ref[...] = jnp.concatenate([a_ref[...], b_ref[...]], axis=1)


def join(a, b):
    return pl.pallas_call(
        join_kernel,
        out_shape=jax.ShapeDtypeStruct((1, a.shape[1] + b.shape[1]), a.dtype),
        in_specs=[VMEM] * 2,
        out_specs=VMEM,
        compiler_params=SMALL,
        name="join",
    )(a, b)


def absorb_kernel(count, *refs):
    queries, (w_ref, _, a_ref, r_ref) = refs[:count], refs[count:]
    half = a_ref.shape[1] // 2
    step = 2 * half // PAIRS
    for duo in range(PAIRS // 2):
        found = []
        for pair in (2 * duo, 2 * duo + 1):
            cols = slice(pair * 2 * DN, (pair + 1) * 2 * DN)
            lhs = [diagonal(q[:, cols].astype(jnp.float32)) for q in queries]
            lhs = jnp.concatenate(lhs, axis=0).astype(jnp.bfloat16)
            found.append(
                lax.dot_general(
                    lhs, w_ref[:, cols], (((1,), (1,)), ((), ())), preferred_element_type=jnp.float32
                )
            )
        rows = slice(duo * step, (duo + 1) * step)
        low_rows = slice(half + duo * step, half + (duo + 1) * step)
        small = step // 2
        for g in range(count):
            own = slice(g * small, (g + 1) * small)
            high, low = split(jnp.concatenate([f[own] for f in found], axis=0))
            a_ref[g, rows] = high.astype(jnp.bfloat16)
            a_ref[g, low_rows] = low.astype(jnp.bfloat16)
            turned = []
            for pair in (2 * duo, 2 * duo + 1):
                cols = slice(H * DN + pair * 2 * DR, H * DN + (pair + 1) * 2 * DR)
                turned.append(diagonal(queries[g][:, cols].astype(jnp.float32)))
            r_ref[g, rows] = jnp.concatenate(turned, axis=0).astype(jnp.bfloat16)


def absorb(queries, w_uk, started):
    count = len(queries)
    rows = queries[0].shape[0] * H
    return pl.pallas_call(
        functools.partial(absorb_kernel, count),
        out_shape=(
            jax.ShapeDtypeStruct((count, 2 * rows, R), jnp.bfloat16),
            jax.ShapeDtypeStruct((count, rows, 2 * DR), jnp.bfloat16),
        ),
        in_specs=[VMEM] * (count + 2),
        out_specs=(VMEM, VMEM),
        compiler_params=PARAMS,
        name="absorb",
    )(*queries, w_uk, started)


def attend_kernel(near, count, first, me_ref, a_ref, r_ref, w_ref, *refs):
    queries, keys = refs[:count], refs[count : count + near]
    docs, outs = refs[count + near : -count], refs[-count:]
    rows = r_ref.shape[1]
    own = queries[0].shape[0]
    eight = 2 * own
    tokens = keys[0].shape[1]
    scale = 1.0 / math.sqrt(DN + DR)
    me = me_ref[0]
    group = range(count)

    spot = iota((eight, META), 0) % own
    lane = iota((eight, META), 1)
    limits = []
    for q in queries:
        meta = q[:1, H * (DN + DR) :].astype(jnp.float32)
        values = [
            jnp.sum(jnp.where(lane == spot + i * own, meta, 0.0), axis=1, keepdims=True)
            for i in range(3)
        ]
        limits.append((values[0], values[1] * 256.0 + values[2]))

    absorbed = jnp.concatenate([a_ref[first + g] for g in group], axis=0)
    turned = jnp.concatenate([r_ref[first + g] for g in group], axis=0)
    scores = [[] for _ in group]
    for k in range(near):
        latent = keys[k][:R, :]
        rope = keys[k][R:, :]
        both = jnp.dot(absorbed, latent, preferred_element_type=jnp.float32)
        turn = jnp.dot(
            turned, jnp.concatenate([rope, rope], axis=0), preferred_element_type=jnp.float32
        )
        place = lax.bitwise_xor(me, k) * tokens + iota((eight, tokens), 1)
        doc = docs[k // 2][:, (k % 2) * tokens : (k % 2 + 1) * tokens].astype(jnp.float32)
        for g in group:
            q_doc, q_pos = limits[g]
            visible = (doc == q_doc) & (place.astype(jnp.float32) <= q_pos)
            top = 2 * g * rows
            found = both[top : top + rows] + both[top + rows : top + 2 * rows]
            found = (found + turn[g * rows : (g + 1) * rows]) * scale
            found = found.reshape(rows // eight, eight, tokens)
            scores[g].append(jnp.where(visible[None], found, HIDDEN).reshape(rows, tokens))
    bests, totals = [], []
    for g in group:
        best = functools.reduce(jnp.maximum, scores[g])
        bests.append(jnp.maximum(jnp.max(best, axis=1, keepdims=True), FLOOR))
    mixed = None
    sums = [None for _ in group]
    for k in range(near):
        both = []
        for g in group:
            weights = jnp.exp(scores[g][k] - bests[g])
            sums[g] = weights if sums[g] is None else sums[g] + weights
            both += split(weights)
        both = jnp.concatenate(both, axis=0).astype(jnp.bfloat16)
        part = lax.dot_general(
            both, keys[k][:R, :], (((1,), (1,)), ((), ())), preferred_element_type=jnp.float32
        )
        mixed = part if mixed is None else mixed + part
    totals = [jnp.sum(s, axis=1, keepdims=True) for s in sums]
    halves = []
    for g in group:
        top = 2 * g * rows
        halves += split(mixed[top : top + rows] + mixed[top + rows : top + 2 * rows])
    stats = [jnp.zeros((eight, META), jnp.float32) for _ in group]
    for pair in range(PAIRS):
        take = slice(pair * eight, (pair + 1) * eight)
        cols = slice(pair * 2 * DV, (pair + 1) * 2 * DV)
        lhs = jnp.concatenate([h[take] for h in halves], axis=0).astype(jnp.bfloat16)
        res = jnp.dot(lhs, w_ref[:, cols], preferred_element_type=jnp.float32)
        for g in group:
            top = 2 * g * eight
            part = res[top : top + eight] + res[top + eight : top + 2 * eight]
            outs[g][:, cols] = jnp.concatenate([part[:own, :DV], part[own:, DV:]], axis=1)
            for base, value in ((0, bests[g]), (2 * PAIRS, totals[g])):
                at = base + pair + jnp.where(iota((eight, META), 0) < own, 0, PAIRS)
                stats[g] = jnp.where(lane == at, value[take], stats[g])
    for g in group:
        outs[g][:, H * DV :] = stats[g][:own] + stats[g][own:]


def attend(me, first, absorbed, turned, queries, w_uv, keys, docs):
    near, count = len(keys), len(queries)
    part = jax.ShapeDtypeStruct((queries[0].shape[0], H * DV + META), jnp.float32)
    return pl.pallas_call(
        functools.partial(attend_kernel, near, count, first),
        out_shape=(part,) * count,
        in_specs=[SMEM] + [VMEM] * (3 + count + near + len(docs)),
        out_specs=(VMEM,) * count,
        compiler_params=PARAMS,
        name="attend",
    )(me, absorbed, turned, w_uv, *queries, *keys, *docs)


def weigh(parts):
    stats = [p[:, H * DV :] for p in parts]
    maxima = [s[:, :H] for s in stats]
    top = functools.reduce(jnp.maximum, maxima)
    factors = [jnp.exp(m - top) for m in maxima]
    total = functools.reduce(jnp.add, [f * s[:, H : 2 * H] for f, s in zip(factors, stats)])
    return top, factors, total


def blend(parts, factors, head):
    lane = (head % 2) * PAIRS + head // 2
    cols = slice(head * DV, (head + 1) * DV)
    rows = parts[0].shape[0]
    found = None
    for i in range(0, len(parts), 2):
        pair = jnp.concatenate([p[:, cols] for p in parts[i : i + 2]], axis=0)
        factor = jnp.concatenate(factors[i : i + 2], axis=0)[:, lane : lane + 1]
        term = pair * factor
        halves = [term[j : j + rows] for j in range(0, term.shape[0], rows)]
        term = functools.reduce(jnp.add, halves)
        found = term if found is None else found + term
    return found


def merge_kernel(count, *refs):
    parts, out_ref = refs[:count], refs[count]
    top, factors, total = weigh(parts)
    for head in range(H):
        out_ref[:, head * DV : (head + 1) * DV] = blend(parts, factors, head)
    rest = jnp.zeros((out_ref.shape[0], META - 2 * H), jnp.float32)
    out_ref[:, H * DV :] = jnp.concatenate([top, total, rest], axis=1)


def merge(parts):
    return pl.pallas_call(
        functools.partial(merge_kernel, len(parts)),
        out_shape=jax.ShapeDtypeStruct(parts[0].shape, jnp.float32),
        in_specs=[VMEM] * len(parts),
        out_specs=VMEM,
        compiler_params=PARAMS,
        name="merge",
    )(*parts)


def combine_kernel(count, *refs):
    parts, out_ref = refs[:count], refs[count]
    _, factors, total = weigh(parts)
    factors = [f / total for f in factors]
    for head in range(H):
        value = blend(parts, factors, head)
        out_ref[:, head * DV : (head + 1) * DV] = value.astype(out_ref.dtype)


def combine(parts):
    return pl.pallas_call(
        functools.partial(combine_kernel, len(parts)),
        out_shape=jax.ShapeDtypeStruct((parts[0].shape[0], H * DV), jnp.bfloat16),
        in_specs=[VMEM] * len(parts),
        out_specs=VMEM,
        compiler_params=PARAMS,
        name="combine",
    )(*parts)


def shards(size, query_nope, query_rope, cache, key_docs, query_docs, query_pos, w_uk, w_uv):
    near = math.gcd(size, 4)
    far = size // near
    me = lax.axis_index("col")

    def swap(x, mask):
        return lax.ppermute(x, "col", [(i, i ^ mask) for i in range(size)])

    block, doc = cache.T, key_docs.reshape(1, -1)
    keys, docs = {0: block}, [doc]
    if near == 4:
        keys[2] = swap(block, 2)
    if near > 1:
        keys[1] = swap(block, 1)
        docs = [join(doc, swap(doc, 1))]
    first = lead(LEAD)
    mine = pack(first, query_docs, query_pos, query_nope, query_rope)
    groups = [mine]
    for k in range(1, far):
        groups.append(swap(mine, near * k))
    if near == 4:
        docs.append(swap(docs[0], 2))
        keys[3] = swap(keys[2], 1)
    keys = [keys[k] for k in range(near)]
    started = lead(4 * LEAD)
    where = jnp.reshape(me, (1,)).astype(jnp.int32)
    parts = [None] * far
    for start in range(0, far, 4):
        some = groups[start : start + 4]
        absorbed, turned = absorb(some, w_uk, started)
        cuts = [(2, len(some)), (1, 2), (0, 1)] if start == 0 else [(0, len(some))]
        for first, end in cuts:
            if first >= end:
                continue
            pick = some[first:end]
            found = attend(where, first, absorbed, turned, pick, w_uv, keys, docs)
            for g, part in enumerate(found):
                k = start + first + g
                parts[k] = part if k == 0 else swap(part, near * k)
    if far > 2:
        parts = [merge(parts[:1] + parts[2:]), parts[1]]
    return combine(parts)


def solution(mesh):
    split_rows = P(("ga", "col"), None)
    split_flat = P(("ga", "col"))
    placed = (split_rows, split_rows, split_rows, split_flat, split_flat, split_flat, P(), P())
    size = mesh.shape["col"]

    def body(*arrays):
        return shards(size, *arrays)

    return jax.shard_map(body, mesh=mesh, in_specs=placed, out_specs=split_rows, check_vma=False)
```
